512 devices in a mesh: ctx: 64 (over y, z), head: 8 (over x, core).
Axes of the slice: x: 4, y: 4, z: 16, core: 2. Of those that a mesh axis runs over, the one named last changes fastest.
Arguments:
- tokens: bfloat16 [16384, 2048], P('ctx'), may hold values from -16 to 16
- queries: float32 [16384, 1024], P('ctx', 'head'), may hold values from -6 to 6
- values: float32 [16384, 1024], P('ctx', 'head'), may hold values from -6 to 6
- dout: float32 [16384, 1024], P('ctx', 'head'), may hold values from -6 to 6
- key_weight: bfloat16 [2048, 4, 1024], P('ctx', None, 'head'), may hold values from -0.125 to 0.125
- routing: int32 [16384, 2], P('ctx'), may hold values from 0 to 3, all different within a row
- gates: float32 [16384, 2], P('ctx'), may hold values from 0.25 to 1
Outputs:
- key_grad: float32 [2048, 4, 1024], P('ctx', None, 'head')
- query_grad: float32 [16384, 1024], P('ctx', 'head')
- value_grad: float32 [16384, 1024], P('ctx', 'head')
- gate_grad: float32 [16384, 2], P('ctx')
The draws below stay inside these ranges and needn't reach their ends.
Inputs may be any that keep to these rules, and one draw needn't show every extreme that they name: `routing`: each row names 2 different memories.
All inputs are finite; a program needn't handle non-finite values.
Results may differ from the reference program's by a relative error of at most 0.0029.
Values may be sent and summed in bfloat16 or wider, within the bound.
A program may use at most 128 MiB of HBM per device.

```python
import math
import jax
import jax.numpy as jnp
from jax import lax

D = 2048
HD = 128
MEM = 4
TOP = 2
TOK_DEV = 256
HW = 1024
TOKENS = 16384


def spiked(result, rng, source, target, parts, factor):
    def block_of(axis_at):
        return (jnp.arange(result.shape[axis_at]) // (result.shape[axis_at] // parts)).reshape((-1,) + (1,) * (result.ndim - 1 - axis_at))

    first = jax.random.permutation(rng, parts)[block_of(target)]
    other_side = (block_of(target) + parts // 2) % parts
    return jnp.where((block_of(source) == first) | (block_of(source) == other_side), factor * result, result)


def block_scale(rng, shape, pieces, least, top_value):
    def one(dim, shards_of):
        heights = jax.random.uniform(jax.random.fold_in(jax.random.fold_in(rng, 6), dim), (shards_of,), jnp.float32, least / len(pieces), top_value / len(pieces))
        return jnp.repeat(jnp.exp(heights), shape[dim] // shards_of).reshape((-1,) + (1,) * (len(shape) - dim - 1))

    gain = one(*pieces[0])
    for cut in pieces[1:]:
        gain = gain * one(*cut)
    return gain


def choose_distinct(stream_key, rows, number_of, top, lift):
    sequence = jax.random.permutation(jax.random.fold_in(stream_key, 1), number_of)
    boost = sequence
    for power in range(3):
        boost = boost * boost // number_of
    boost = boost * lift // number_of
    tickets = jax.random.randint(jax.random.fold_in(stream_key, 2), (rows, number_of), 0, 4096) + boost
    holders = jax.random.permutation(jax.random.fold_in(stream_key, 3), rows)[jnp.arange(number_of) % rows]
    tickets = jnp.where(jnp.arange(rows)[:, None] == holders[None, :], 1 << 14, tickets)
    priority = tickets * number_of + jnp.arange(number_of)
    return lax.top_k(priority.astype(jnp.int32), top)[1].astype(jnp.int32)


def gaussian(own_key, dims, deviation, bound, shards=(), held_as=jnp.bfloat16):
    gain = block_scale(own_key, dims, shards, -0.22, 0.18) if shards else 1.0
    result = jax.random.normal(own_key, dims, jnp.float32) * deviation * gain
    return jnp.minimum(jnp.maximum(result, -bound), bound).astype(held_as)


def gaussian_with(rng, dims, spread, reach, cuts, heavy, kind=jnp.bfloat16):
    array = spread * jax.random.normal(rng, dims, jnp.float32)
    if cuts:
        array = array * block_scale(rng, dims, cuts, -0.22, 0.18)
    return jnp.clip(spiked(array, jax.random.fold_in(rng, 3), *heavy), -reach, reach).astype(kind)


def setup_inputs(seed: int = 0) -> dict:
    seeds = jax.random.split(jax.random.key(seed), 8)
    return {
        "tokens": gaussian_with(seeds[0], (TOKENS, D), 1.0, 16.0, ((0, 64),), (0, 1, 64, 4.0)),
        "queries": gaussian(seeds[1], (TOKENS, HW), 1.0, 6.0, ((0, 64), (1, 8)), jnp.float32),
        "values": gaussian(seeds[2], (TOKENS, HW), 1.0, 6.0, ((0, 64), (1, 8)), jnp.float32),
        "dout": gaussian(seeds[3], (TOKENS, HW), 1.0, 6.0, ((0, 64), (1, 8)), jnp.float32),
        "key_weight": gaussian(seeds[4], (D, MEM, HW), D ** -0.5, 0.125, ((0, 64), (2, 8))),
        "routing": choose_distinct(seeds[5], TOKENS, MEM, TOP, 4096),
        "gates": jnp.clip(0.25 + 0.75 * jax.random.uniform(seeds[6], (TOKENS, TOP), jnp.float32) ** block_scale(seeds[6], (TOKENS, TOP), ((0, 64),), -0.2, 0.2), 0.25, 1.0),
    }


def routing_tables(routing, gates, memories):
    onehot = (routing[:, :, None] == jnp.arange(memories, dtype=jnp.int32)[None, None, :]).astype(jnp.float32)
    routed = lax.optimization_barrier(jnp.sum(onehot, axis=1))
    weighted = lax.optimization_barrier(jnp.sum(gates[:, :, None] * onehot, axis=1))
    return (routed, weighted, onehot)

def block_states(queries, values, dout, keys, routed, weighted, scale):
    highest = lax.Precision.HIGHEST
    masked_keys = keys * routed[:, :, None]
    key_local = jnp.einsum('tmk,tv->mkv', masked_keys, values, precision=highest)
    lifted = weighted[:, :, None] * queries[:, None, :]
    grad_local = scale * jnp.einsum('tmk,tv->mkv', lifted, dout, precision=highest)
    return (key_local, grad_local)

def block_grads(queries, values, dout, keys, routed, weighted, key_in, grad_in, scale):
    highest = lax.Precision.HIGHEST
    count = queries.shape[0]
    memories = keys.shape[1]
    head_dim = keys.shape[2]
    places = jnp.arange(count, dtype=jnp.int32)
    causal = (places[:, None] >= places[None, :]).astype(jnp.float32)
    masked_keys = keys * routed[:, :, None]
    scores = jnp.dot(dout, values.T, precision=highest) * causal
    carried_q = jnp.einsum('tv,mkv->tmk', dout, key_in, precision=highest)
    inner_q = jnp.dot(scores, masked_keys.reshape(count, memories * head_dim), precision=highest).reshape(count, memories, head_dim)
    state_dout = carried_q + inner_q
    query_grad = scale * jnp.einsum('tm,tmk->tk', weighted, state_dout, precision=highest)
    gate_part = scale * jnp.einsum('tk,tmk->tm', queries, state_dout, precision=highest)
    lifted = (weighted[:, :, None] * queries[:, None, :]).reshape(count, memories * head_dim)
    carried_k = jnp.einsum('tv,mkv->tmk', values, grad_in, precision=highest)
    inner_k = scale * jnp.dot(scores.T, lifted, precision=highest).reshape(count, memories, head_dim)
    key_part = routed[:, :, None] * (carried_k + inner_k)
    carried_v = jnp.einsum('tmk,mkv->tv', masked_keys, grad_in, precision=highest)
    products = jnp.einsum('sk,tmk->mst', queries, masked_keys, precision=highest)
    mixed = jnp.einsum('mst,sm->st', products, weighted, precision=highest) * causal
    value_grad = carried_v + scale * jnp.dot(mixed.T, dout, precision=highest)
    return (query_grad, key_part, value_grad, gate_part)

def reference(tokens, queries, values, dout, key_weight, routing, gates):
    total = tokens.shape[0]
    width = tokens.shape[1]
    memories = key_weight.shape[1]
    heads = queries.shape[1] // HD
    blocks = total // TOK_DEV
    scale = 1.0 / math.sqrt(HD * TOKENS)
    routed, weighted, onehot = routing_tables(routing, gates, memories)
    routed_blocks = routed.reshape(blocks, TOK_DEV, memories)
    weighted_blocks = weighted.reshape(blocks, TOK_DEV, memories)

    def per_head(inputs):
        head_queries, head_values, head_dout, head_weight = inputs
        keys = jnp.dot(tokens, head_weight.reshape(width, memories * HD), preferred_element_type=jnp.float32)
        keys_blocks = keys.reshape(blocks, TOK_DEV, memories, HD)
        query_blocks = head_queries.reshape(blocks, TOK_DEV, HD)
        value_blocks = head_values.reshape(blocks, TOK_DEV, HD)
        dout_blocks = head_dout.reshape(blocks, TOK_DEV, HD)
        states_fn = jax.vmap(lambda q, v, d, k, r, w: block_states(q, v, d, k, r, w, scale))
        key_local, grad_local = states_fn(query_blocks, value_blocks, dout_blocks, keys_blocks, routed_blocks, weighted_blocks)
        key_in = jnp.cumsum(key_local, axis=0) - key_local
        grad_in = lax.optimization_barrier(jnp.sum(grad_local, axis=0)) - jnp.cumsum(grad_local, axis=0)
        grads_fn = jax.vmap(lambda q, v, d, k, r, w, a, b: block_grads(q, v, d, k, r, w, a, b, scale))
        query_grad, key_part, value_grad, gate_part = grads_fn(query_blocks, value_blocks, dout_blocks, keys_blocks, routed_blocks, weighted_blocks, key_in, grad_in)
        key_low = key_part.reshape(total, memories * HD).astype(jnp.bfloat16)
        weight_grad = lax.dot_general(tokens, key_low, (((0,), (0,)), ((), ())), preferred_element_type=jnp.float32)
        return (query_grad.reshape(total, HD), value_grad.reshape(total, HD), weight_grad.reshape(width, memories, HD), gate_part.reshape(total, memories))
    query_heads = queries.reshape(total, heads, HD).transpose(1, 0, 2)
    value_heads = values.reshape(total, heads, HD).transpose(1, 0, 2)
    dout_heads = dout.reshape(total, heads, HD).transpose(1, 0, 2)
    weight_heads = key_weight.reshape(width, memories, heads, HD).transpose(2, 0, 1, 3)
    query_all, value_all, weight_all, gate_all = lax.map(per_head, (query_heads, value_heads, dout_heads, weight_heads))
    query_grad = query_all.transpose(1, 0, 2).reshape(total, heads * HD)
    value_grad = value_all.transpose(1, 0, 2).reshape(total, heads * HD)
    key_grad = weight_all.transpose(1, 2, 0, 3).reshape(width, memories, heads * HD)
    gate_sum = lax.optimization_barrier(jnp.sum(gate_all, axis=0))
    gate_grad = jnp.einsum('tjm,tm->tj', onehot, gate_sum, precision=lax.Precision.HIGHEST)
    return (key_grad, query_grad, value_grad, gate_grad)
```

```python
import functools
import math

import jax
import jax.numpy as jnp
from jax import lax
from jax.experimental import pallas as pl
from jax.experimental.pallas import tpu as pltpu
from jax.sharding import PartitionSpec as P

MESH = pl.DeviceIdType.MESH
F32 = jnp.float32
BF16 = jnp.bfloat16
NN = (((1,), (0,)), ((), ()))
NT = (((1,), (1,)), ((), ()))


def split(x):
    high = x.astype(BF16)
    return high, (x - high.astype(F32)).astype(BF16)


def dot(a, b, dims):
    return lax.dot_general(a, b, dims, preferred_element_type=F32)


def dot3(a, b, dims):
    return dot(a[0], b[0], dims) + (dot(a[0], b[1], dims) + dot(a[1], b[0], dims))


def each(lower, upper, body):
    def step(i, carry):
        body(i)
        return carry

    lax.fori_loop(lower, upper, step, 0)


def kernel(
    sizes,
    tok, q_ref, v_ref, do_ref, w_ref, r_ref, g_ref,
    kg_out, qg_out, vg_out, gg_out,
    wall, tk, tkt, kgl, kgl_in, lift_h, lift_l, mk_h, mk_l, cols,
    gsend, gin, gmid, gtot, gback, gcar,
    ksend, kin, kmid, ktot, kback, kcar,
    prod, stage, land, gate, gate_in,
    sc_h, sc_l, inner,
    ww_s, ww_r, wy_s, wy_r, ty_s, ty_r, th_s, th_r,
    ga_s, ga_r, gt_s, gt_r, gb_s, gb_r,
    ka_s, ka_r, kt_s, kt_r, kb_s, kb_r,
    ky_s, ky_r, rs_s, rs_r, gp_s, gp_r,
):
    ny, nz, nh, mem, hd, scale = sizes
    ctx, head = lax.axis_index("ctx"), lax.axis_index("head")
    my_y, my_z = ctx // nz, ctx % nz
    count, width = tok.shape
    wide = mem * hd
    part = count // nh
    lane = width // ny
    right_hops, left_hops = nz // 2 - 1, nz // 2

    def at_z(z):
        return {"ctx": my_y * nz + lax.rem(z + 2 * nz, nz)}

    def at_y(y):
        return {"ctx": lax.rem(y + ny, ny) * nz + my_z}

    def at_head(h):
        return {"head": lax.rem(h, nh)}

    def copy(src, dst, send, recv, to):
        return pltpu.make_async_remote_copy(
            src_ref=src, dst_ref=dst, send_sem=send, recv_sem=recv,
            device_id=to, device_id_type=MESH,
        )

    barrier = pltpu.get_barrier_semaphore()

    def greet(to):
        pl.semaphore_signal(barrier, inc=1, device_id=to, device_id_type=MESH)

    each(1, nz, lambda d: greet(at_z(my_z + d)))
    each(1, ny, lambda d: greet(at_y(my_y + d)))
    each(1, nh, lambda d: greet(at_head(head + d)))

    row = lax.broadcasted_iota(jnp.int32, (128, count), 0)
    memory, group = row % mem, row // mem
    first = (r_ref[0:1, :] == memory).astype(F32)
    second = (r_ref[1:2, :] == memory).astype(F32)
    weights = g_ref[0:1, :] * first + g_ref[1:2, :] * second
    table = jnp.where(
        group == 0, weights,
        jnp.where(group == 1, first + second, jnp.where(group == 2, first, jnp.where(group == 3, second, 0.0))),
    )
    cols[...] = table.T

    def column(kind, m):
        return cols[:, kind * mem + m : kind * mem + m + 1]

    scaled_q = q_ref[...] * scale
    for m in range(mem):
        high, low = split(column(0, m) * scaled_q)
        lift_h[:, m * hd : (m + 1) * hd] = high
        lift_l[:, m * hd : (m + 1) * hd] = low

    dout2 = split(do_ref[...])
    dout_t = split(do_ref[...].T)
    local = dot3(dout_t, (lift_h[...], lift_l[...]), NN)
    gsend[...] = local.reshape(gsend.shape)

    pl.semaphore_wait(barrier, (nz - 1) + (ny - 1) + (nh - 1))

    def ring_right(k, src=None):
        at = my_y * nz + lax.rem(my_z - (k - 1) + nz, nz)
        src = wall.at[at] if src is None else src
        return copy(src, wall.at[at], ww_s.at[0, k - 1], ww_r.at[0, k - 1], at_z(my_z + 1))

    def ring_left(k, src=None):
        at = my_y * nz + lax.rem(my_z + (k - 1), nz)
        src = wall.at[at] if src is None else src
        return copy(src, wall.at[at], ww_s.at[1, k - 1], ww_r.at[1, k - 1], at_z(my_z - 1))

    def to_rows(z, src=None):
        at = my_y * nz + lax.rem(z + 2 * nz, nz)
        for d in range(1, ny):
            copy(
                wall.at[at] if src is None else src, wall.at[at],
                wy_s.at[d - 1], wy_r.at[d - 1], at_y(my_y + d),
            ).start()

    def scan_out(src, dst, send, recv, d):
        z = lax.rem(my_z + d, nz)
        return copy(src.at[z], dst.at[my_z], send.at[d - 1], recv.at[d - 1], at_z(z))

    ring_right(1, w_ref).start()
    ring_left(1, w_ref).start()
    each(1, nz, lambda d: scan_out(gsend, gin, ga_s, ga_r, d).start())

    def token_rows(d):
        y = lax.rem(my_y + d, ny)
        rows = pl.ds(pl.multiple_of(head * part, part), part)
        return copy(
            tok.at[rows, pl.ds(pl.multiple_of(y * lane, lane), lane)],
            tk.at[d - 1, rows], ty_s.at[d - 1], ty_r.at[d - 1], at_y(y),
        )

    for d in range(1, ny):
        token_rows(d).start()
    to_rows(my_z, w_ref)
    wall[ctx] = w_ref[...]
    gin[my_z] = gsend[my_z]

    def ring_step(k):
        ring_right(k).wait_recv()
        ring_right(k + 1).start()
        ring_left(k).wait_recv()

        @pl.when(k < right_hops)
        def _():
            ring_left(k + 1).start()

        to_rows(my_z - k)
        to_rows(my_z + k)

    each(1, right_hops + 1, ring_step)
    ring_right(left_hops).wait_recv()
    to_rows(my_z - left_hops)

    def token_share(d):
        rows = pl.ds(pl.multiple_of(head * part, part), part)
        return copy(tk.at[:, rows], tk.at[:, rows], th_s.at[d - 1], th_r.at[d - 1], at_head(head + d))

    for d in range(1, ny):
        token_rows(d).wait_recv()
    each(1, nh, lambda d: token_share(d).start())

    def scan_middle(src, tot, send, recv, d):
        return copy(src, tot.at[d - 1], send.at[d - 1], recv.at[d - 1], at_y(my_y + d))

    def sweep(inbox, mid, backwards):
        total = jnp.zeros(inbox.shape[1:], F32)
        for z in reversed(range(nz)) if backwards else range(nz):
            mid[z] = total
            total = total + inbox[z]
        return total

    def spread(tot, mid, backwards):
        extra = jnp.zeros(tot.shape[1:], F32)
        for d in range(1, ny):
            y = lax.rem(my_y - d + ny, ny)
            reached = (y > my_y) if backwards else (y < my_y)
            extra = extra + tot[d - 1] * reached.astype(F32)
        for z in range(nz):
            mid[z] = mid[z] + extra

    each(1, nz, lambda d: scan_out(gsend, gin, ga_s, ga_r, d).wait_recv())
    gback[...] = sweep(gin, gmid, True)
    for d in range(1, ny):
        scan_middle(gback, gtot, gt_s, gt_r, d).start()

    places_s = lax.broadcasted_iota(jnp.int32, (count, count), 0)
    places_t = lax.broadcasted_iota(jnp.int32, (count, count), 1)
    val2 = split(v_ref[...])
    scores = jnp.where(places_s >= places_t, dot3(dout2, val2, NT), 0.0)
    sc_h[...], sc_l[...] = split(scores)
    scores_t = split(jnp.where(places_t >= places_s, dot3(val2, dout2, NT), 0.0))

    for d in range(1, ny):
        scan_middle(gback, gtot, gt_s, gt_r, d).wait_recv()
    spread(gtot, gmid, True)
    each(1, nz, lambda d: scan_out(gmid, gcar, gb_s, gb_r, d).start())
    gcar[my_z] = gmid[my_z]
    inner[...] = dot3(scores_t, (lift_h[...], lift_l[...]), NN)

    each(1, nz, lambda d: scan_out(gmid, gcar, gb_s, gb_r, d).wait_recv())
    gcar2 = split(gcar[...].reshape(hd, wide))
    carried_k = dot3(val2, gcar2, NN)
    for m in range(mem):
        at = slice(m * hd, (m + 1) * hd)
        kgl[:, at] = (column(1, m) * (carried_k[:, at] + inner[:, at])).astype(BF16)

    def key_rows(d):
        return copy(kgl, kgl_in.at[d - 1], ky_s.at[d - 1], ky_r.at[d - 1], at_y(my_y + d))

    for d in range(1, ny):
        key_rows(d).start()

    def row_pieces(d):
        y = lax.rem(my_y - d + ny, ny)
        at = pl.ds(y * nz, nz)
        return copy(wall.at[at], wall.at[at], wy_s.at[d - 1], wy_r.at[d - 1], at_y(my_y + d))

    for d in range(1, ny):
        row_pieces(d).wait_recv()
    keys = dot(tok[...], wall[...].reshape(width, wide), NN)
    for m in range(mem):
        at = slice(m * hd, (m + 1) * hd)
        mk_h[:, at], mk_l[:, at] = split(column(1, m) * keys[:, at])
    mk2 = (mk_h[...], mk_l[...])
    val_t = split(v_ref[...].T)
    ksend[...] = dot3(val_t, mk2, NN).reshape(ksend.shape)
    each(1, nz, lambda d: scan_out(ksend, kin, ka_s, ka_r, d).start())
    kin[my_z] = ksend[my_z]

    each(1, nh, lambda d: token_share(d).wait_recv())
    own_lanes = pl.ds(pl.multiple_of(my_y * lane, lane), lane)
    tkt[:, 0:count] = tok[:, own_lanes].T
    for d in range(1, ny):
        tkt[:, d * count : (d + 1) * count] = tk[d - 1].T

    each(1, nz, lambda d: scan_out(ksend, kin, ka_s, ka_r, d).wait_recv())
    kback[...] = sweep(kin, kmid, False)
    for d in range(1, ny):
        scan_middle(kback, ktot, kt_s, kt_r, d).start()

    for d in range(1, ny):
        key_rows(d).wait_recv()
    product = dot(tkt[:, 0:count], kgl[...], NN)
    for d in range(1, ny):
        product = product + dot(tkt[:, d * count : (d + 1) * count], kgl_in[d - 1], NN)
    for m in range(mem):
        prod[:, m] = product[:, m * hd : (m + 1) * hd].reshape(nz, width // ny // nz, hd)

    def flow(side, s, m):
        to = at_z(my_z + 1) if side == 0 else at_z(my_z - 1)
        return copy(
            stage.at[side, s - 1, m], land.at[side, s - 1, m],
            rs_s.at[side, s - 1, m], rs_r.at[side, s - 1, m], to,
        )

    def target(side, s):
        if side == 0:
            return lax.rem(my_z + right_hops + 1 - s, nz)
        return lax.rem(my_z - left_hops - 1 + s + 2 * nz, nz)

    for side in range(2):
        for m in range(mem):
            stage[side, 0, m] = prod[target(side, 1), m]
            flow(side, 1, m).start()

    for d in range(1, ny):
        scan_middle(kback, ktot, kt_s, kt_r, d).wait_recv()
    spread(ktot, kmid, False)
    each(1, nz, lambda d: scan_out(kmid, kcar, kb_s, kb_r, d).start())
    kcar[my_z] = kmid[my_z]

    def reduce_step(s):
        for m in range(mem):
            for side in range(2):
                flow(side, s - 1, m).wait_recv()
                stage[side, s - 1, m] = land[side, s - 2, m] + prod[target(side, s), m]
                flow(side, s, m).start()

    def early(s):
        reduce_step(s)

    middle = min(3, right_hops)
    each(2, middle + 1, early)

    mixed = jnp.where(places_t >= places_s, dot3(mk2, (lift_h[...], lift_l[...]), NT), 0.0)
    vg_out[...] = dot3(mk2, split(gcar[...].reshape(hd, wide)), NT) + dot3(split(mixed), dout2, NN)

    each(middle + 1, right_hops + 1, early)

    each(1, nz, lambda d: scan_out(kmid, kcar, kb_s, kb_r, d).wait_recv())
    state = dot3(dout2, split(kcar[...].reshape(hd, wide)), NN) + dot3((sc_h[...], sc_l[...]), mk2, NN)
    scaled_q = q_ref[...] * scale
    query = jnp.zeros((count, hd), F32)
    picks = [jnp.zeros((count, 1), F32), jnp.zeros((count, 1), F32)]
    for m in range(mem):
        here = state[:, m * hd : (m + 1) * hd]
        query = query + column(0, m) * here
        gradient = jnp.sum(scaled_q * here, axis=1, keepdims=True)
        for j in range(2):
            picks[j] = picks[j] + column(2 + j, m) * gradient
    qg_out[...] = scale * query
    lanes = lax.broadcasted_iota(jnp.int32, (count, hd), 1)
    spreaded = jnp.where(lanes == 0, picks[0], jnp.where(lanes == 1, picks[1], 0.0))
    gate[...] = spreaded.T[0:8, :]

    def gate_share(d):
        return copy(gate, gate_in.at[d - 1], gp_s.at[d - 1], gp_r.at[d - 1], at_head(head + d))

    each(1, nh, lambda d: gate_share(d).start())

    for m in range(mem):
        flow(1, left_hops - 1, m).wait_recv()
        stage[1, left_hops - 1, m] = land[1, left_hops - 2, m] + prod[target(1, left_hops), m]
        flow(1, left_hops, m).start()

    each(1, nh, lambda d: gate_share(d).wait_recv())
    total = gate[...]
    for d in range(1, nh):
        total = total + gate_in[d - 1]
    gg_out[...] = total[0:2, :]

    for m in range(mem):
        flow(0, right_hops, m).wait_recv()
        flow(1, left_hops, m).wait_recv()
        kg_out[:, m * hd : (m + 1) * hd] = (
            prod[my_z, m] + land[0, right_hops - 1, m] + land[1, left_hops - 1, m]
        )

    each(1, left_hops + 1, lambda k: ring_right(k).wait_send())
    each(1, right_hops + 1, lambda k: ring_left(k).wait_send())
    for d in range(1, ny):
        row_pieces(d).wait_send()
        token_rows(d).wait_send()
        scan_middle(gback, gtot, gt_s, gt_r, d).wait_send()
        scan_middle(kback, ktot, kt_s, kt_r, d).wait_send()
        key_rows(d).wait_send()

    def sent(d):
        scan_out(gsend, gin, ga_s, ga_r, d).wait_send()
        scan_out(gmid, gcar, gb_s, gb_r, d).wait_send()
        scan_out(ksend, kin, ka_s, ka_r, d).wait_send()
        scan_out(kmid, kcar, kb_s, kb_r, d).wait_send()

    each(1, nz, sent)

    def shared(d):
        token_share(d).wait_send()
        gate_share(d).wait_send()

    each(1, nh, shared)

    def reduced(s):
        for m in range(mem):
            flow(0, s, m).wait_send()
            flow(1, s, m).wait_send()

    each(1, right_hops + 1, reduced)
    for m in range(mem):
        flow(1, left_hops, m).wait_send()


def on_device(rows, tokens, queries, values, dout, key_weight, routing, gates):
    count, width = tokens.shape
    depth, mem, hd = key_weight.shape
    contexts, nh = lax.axis_size("ctx"), lax.axis_size("head")
    ny, nz = rows, contexts // rows
    wide = mem * hd
    scale = 1.0 / math.sqrt(hd * count * contexts)
    half = nz // 2
    dma = pltpu.SemaphoreType.DMA
    slab = (nz, hd // nz, wide)
    scan = [
        pltpu.VMEM(slab, F32),
        pltpu.VMEM(slab, F32),
        pltpu.VMEM(slab, F32),
        pltpu.VMEM((ny - 1,) + slab[1:], F32),
        pltpu.VMEM(slab[1:], F32),
        pltpu.VMEM(slab, F32),
    ]
    scan_sems = [dma((nz - 1,))] * 2 + [dma((ny - 1,))] * 2 + [dma((nz - 1,))] * 2
    scratch = (
        [
            pltpu.VMEM((contexts, depth, wide), BF16),
            pltpu.VMEM((ny - 1, count, width // ny), BF16),
            pltpu.VMEM((width // ny, ny * count), BF16),
            pltpu.VMEM((count, wide), BF16),
            pltpu.VMEM((ny - 1, count, wide), BF16),
            pltpu.VMEM((count, wide), BF16),
            pltpu.VMEM((count, wide), BF16),
            pltpu.VMEM((count, wide), BF16),
            pltpu.VMEM((count, wide), BF16),
            pltpu.VMEM((count, 128), F32),
        ]
        + scan
        + scan
        + [
            pltpu.VMEM((nz, mem, depth, hd), F32),
            pltpu.VMEM((2, half, mem, depth, hd), F32),
            pltpu.VMEM((2, half, mem, depth, hd), F32),
            pltpu.VMEM((8, count), F32),
            pltpu.VMEM((nh - 1, 8, count), F32),
            pltpu.VMEM((count, count), BF16),
            pltpu.VMEM((count, count), BF16),
            pltpu.VMEM((count, wide), F32),
        ]
        + [dma((2, half))] * 2
        + [dma((ny - 1,))] * 4
        + [dma((nh - 1,))] * 2
        + scan_sems
        + scan_sems
        + [dma((ny - 1,))] * 2
        + [dma((2, half, mem))] * 2
        + [dma((nh - 1,))] * 2
    )
    vmem = pl.BlockSpec(memory_space=pltpu.VMEM)
    key_grad, query_grad, value_grad, gate_grad = pl.pallas_call(
        functools.partial(kernel, (ny, nz, nh, mem, hd, scale)),
        out_shape=(
            jax.ShapeDtypeStruct((depth, wide), F32),
            jax.ShapeDtypeStruct((count, hd), F32),
            jax.ShapeDtypeStruct((count, hd), F32),
            jax.ShapeDtypeStruct((2, count), F32),
        ),
        in_specs=[vmem] * 7,
        out_specs=(vmem,) * 4,
        scratch_shapes=scratch,
        compiler_params=pltpu.CompilerParams(
            collective_id=0, has_side_effects=True, vmem_limit_bytes=56 * 1024 * 1024
        ),
    )(tokens, queries, values, dout, key_weight.reshape(depth, wide), routing.T, gates.T)
    return key_grad.reshape(depth, mem, hd), query_grad, value_grad, gate_grad.T


def solution(mesh, rows=4):
    return jax.shard_map(
        functools.partial(on_device, rows),
        mesh=mesh,
        in_specs=(
            P("ctx", None),
            P("ctx", "head"),
            P("ctx", "head"),
            P("ctx", "head"),
            P("ctx", None, "head"),
            P("ctx", None),
            P("ctx", None),
        ),
        out_specs=(P("ctx", None, "head"), P("ctx", "head"), P("ctx", "head"), P("ctx", None)),
        check_vma=False,
    )
```

```python
import functools
import math

import jax
import jax.numpy as jnp
from jax import lax
from jax.experimental import pallas as pl
from jax.experimental.pallas import tpu as pltpu
from jax.sharding import PartitionSpec as P

MESH = pl.DeviceIdType.MESH
F32 = jnp.float32
BF16 = jnp.bfloat16
NN = (((1,), (0,)), ((), ()))
NT = (((1,), (1,)), ((), ()))


def split(x):
    high = x.astype(BF16)
    return high, (x - high.astype(F32)).astype(BF16)


def dot(a, b, dims):
    return lax.dot_general(a, b, dims, preferred_element_type=F32)


def dot3(a, b, dims):
    return dot(a[0], b[0], dims) + (dot(a[0], b[1], dims) + dot(a[1], b[0], dims))


def each(lower, upper, body):
    def step(i, carry):
        body(i)
        return carry

    lax.fori_loop(lower, upper, step, 0)


def kernel(
    sizes,
    tok_hbm, q_hbm, v_hbm, do_hbm, w_hbm, r_hbm, g_hbm,
    kg_out, qg_out, vg_out, gg_out,
    tok, q_ref, v_ref, do_ref, w_ref, r_ref, g_ref, in_sems,
    wall, tk, tkt, kgl, kgl_in, lift_h, lift_l, mk_h, mk_l, cols,
    gsend, gin, gmid, gtot, gback, gcar,
    ksend, kin, kmid, ktot, kback, kcar, kmid_low,
    prod, stage, land, gate, gate_in,
    sc_h, sc_l, inner, gc_h, gc_l,
    ww_s, ww_r, wy_s, wy_r, ty_s, ty_r, th_s, th_r,
    ga_s, ga_r, gt_s, gt_r, gb_s, gb_r,
    ka_s, ka_r, kt_s, kt_r, kb_s, kb_r,
    ky_s, ky_r, rs_s, rs_r, gp_s, gp_r,
):
    ny, nz, nh, mem, hd, scale = sizes
    ctx, head = lax.axis_index("ctx"), lax.axis_index("head")
    my_y, my_z = ctx // nz, ctx % nz
    count, width = tok.shape
    wide = mem * hd
    part = count // nh
    lane = width // ny
    groups = 2
    group_wide = wide // groups
    right_hops, left_hops = nz // 2 - 1, nz // 2

    def at_z(z):
        return {"ctx": my_y * nz + lax.rem(z + 2 * nz, nz)}

    def at_y(y):
        return {"ctx": lax.rem(y + ny, ny) * nz + my_z}

    def at_head(h):
        return {"head": lax.rem(h, nh)}

    def copy(src, dst, send, recv, to):
        return pltpu.make_async_remote_copy(
            src_ref=src, dst_ref=dst, send_sem=send, recv_sem=recv,
            device_id=to, device_id_type=MESH,
        )

    barrier = pltpu.get_barrier_semaphore()

    def greet(to):
        pl.semaphore_signal(barrier, inc=1, device_id=to, device_id_type=MESH)

    each(1, nz, lambda d: greet(at_z(my_z + d)))
    each(1, ny, lambda d: greet(at_y(my_y + d)))
    each(1, nh, lambda d: greet(at_head(head + d)))

    fetches = [
        pltpu.make_async_copy(src, dst, in_sems.at[i])
        for i, (src, dst) in enumerate(
            [
                (r_hbm, r_ref), (g_hbm, g_ref), (q_hbm, q_ref), (do_hbm, do_ref),
                (v_hbm, v_ref), (w_hbm, w_ref), (tok_hbm, tok),
            ]
        )
    ]
    for fetch in fetches:
        fetch.start()
    for fetch in fetches[:4]:
        fetch.wait()

    row = lax.broadcasted_iota(jnp.int32, (128, count), 0)
    memory, group = row % mem, row // mem
    first = (r_ref[0:1, :] == memory).astype(F32)
    second = (r_ref[1:2, :] == memory).astype(F32)
    weights = g_ref[0:1, :] * first + g_ref[1:2, :] * second
    table = jnp.where(
        group == 0, weights,
        jnp.where(group == 1, first + second, jnp.where(group == 2, first, jnp.where(group == 3, second, 0.0))),
    )
    cols[...] = table.T

    def column(kind, m):
        return cols[:, kind * mem + m : kind * mem + m + 1]

    scaled_q = q_ref[...] * scale
    for m in range(mem):
        high, low = split(column(0, m) * scaled_q)
        lift_h[:, m * hd : (m + 1) * hd] = high
        lift_l[:, m * hd : (m + 1) * hd] = low

    gsend[...] = dot3(split(do_ref[...].T), (lift_h[...], lift_l[...]), NN).reshape(gsend.shape)

    fetches[4].wait()
    fetches[5].wait()
    places_s = lax.broadcasted_iota(jnp.int32, (count, count), 0)
    places_t = lax.broadcasted_iota(jnp.int32, (count, count), 1)
    dout2 = split(do_ref[...])
    val2 = split(v_ref[...])
    scores = jnp.where(places_s >= places_t, dot3(dout2, val2, NT), 0.0)
    sc_h[...], sc_l[...] = split(scores)
    scores_t = split(jnp.where(places_t >= places_s, dot3(val2, dout2, NT), 0.0))
    inner[...] = dot3(scores_t, (lift_h[...], lift_l[...]), NN)
    fetches[6].wait()
    own_lanes = pl.ds(pl.multiple_of(my_y * lane, lane), lane)
    tkt[:, 0:count] = tok[:, own_lanes].T

    pl.semaphore_wait(barrier, (nz - 1) + (ny - 1) + (nh - 1))

    def ring_right(k, src=None):
        at = my_y * nz + lax.rem(my_z - (k - 1) + nz, nz)
        src = wall.at[at] if src is None else src
        return copy(src, wall.at[at], ww_s.at[0, k - 1], ww_r.at[0, k - 1], at_z(my_z + 1))

    def ring_left(k, src=None):
        at = my_y * nz + lax.rem(my_z + (k - 1), nz)
        src = wall.at[at] if src is None else src
        return copy(src, wall.at[at], ww_s.at[1, k - 1], ww_r.at[1, k - 1], at_z(my_z - 1))

    def to_rows(z, src=None):
        at = my_y * nz + lax.rem(z + 2 * nz, nz)
        for d in range(1, ny):
            copy(
                wall.at[at] if src is None else src, wall.at[at],
                wy_s.at[d - 1], wy_r.at[d - 1], at_y(my_y + d),
            ).start()

    def scan_out(src, dst, send, recv, d):
        z = lax.rem(my_z + d, nz)
        return copy(src.at[z], dst.at[my_z], send.at[d - 1], recv.at[d - 1], at_z(z))

    ring_right(1, w_ref).start()
    ring_left(1, w_ref).start()
    each(1, nz, lambda d: scan_out(gsend, gin, ga_s, ga_r, d).start())

    def token_rows(d):
        y = lax.rem(my_y + d, ny)
        rows = pl.ds(pl.multiple_of(head * part, part), part)
        return copy(
            tok.at[rows, pl.ds(pl.multiple_of(y * lane, lane), lane)],
            tk.at[d - 1, rows], ty_s.at[d - 1], ty_r.at[d - 1], at_y(y),
        )

    for d in range(1, ny):
        token_rows(d).start()
    to_rows(my_z, w_ref)
    wall[ctx] = w_ref[...]
    gin[my_z] = gsend[my_z]

    def ring_step(k):
        ring_right(k).wait_recv()
        ring_right(k + 1).start()
        ring_left(k).wait_recv()

        @pl.when(k < right_hops)
        def _():
            ring_left(k + 1).start()

        to_rows(my_z - k)
        to_rows(my_z + k)

    pause = max(right_hops - 2, 1)
    each(1, pause + 1, ring_step)

    def scan_middle(src, tot, send, recv, d):
        return copy(src, tot.at[d - 1], send.at[d - 1], recv.at[d - 1], at_y(my_y + d))

    def sweep(inbox, mid, backwards):
        total = jnp.zeros(inbox.shape[1:], F32)
        for z in reversed(range(nz)) if backwards else range(nz):
            mid[z] = total
            total = total + inbox[z]
        return total

    def extra_of(tot, backwards):
        extra = jnp.zeros(tot.shape[1:], F32)
        for d in range(1, ny):
            y = lax.rem(my_y - d + ny, ny)
            reached = (y > my_y) if backwards else (y < my_y)
            extra = extra + tot[d - 1] * reached.astype(F32)
        return extra

    each(1, nz, lambda d: scan_out(gsend, gin, ga_s, ga_r, d).wait_recv())
    gback[...] = sweep(gin, gmid, True)
    for d in range(1, ny):
        scan_middle(gback, gtot, gt_s, gt_r, d).start()

    def token_share(d):
        rows = pl.ds(pl.multiple_of(head * part, part), part)
        return copy(tk.at[:, rows], tk.at[:, rows], th_s.at[d - 1], th_r.at[d - 1], at_head(head + d))

    for d in range(1, ny):
        token_rows(d).wait_recv()
    each(1, nh, lambda d: token_share(d).start())
    each(pause + 1, right_hops + 1, ring_step)

    for d in range(1, ny):
        scan_middle(gback, gtot, gt_s, gt_r, d).wait_recv()
    extra = extra_of(gtot, True)
    for z in range(nz):
        gmid[z] = gmid[z] + extra
    each(1, nz, lambda d: scan_out(gmid, gcar, gb_s, gb_r, d).start())
    gcar[my_z] = gmid[my_z]

    ring_right(left_hops).wait_recv()
    to_rows(my_z - left_hops)

    def row_pieces(d):
        y = lax.rem(my_y - d + ny, ny)
        at = pl.ds(y * nz, nz)
        return copy(wall.at[at], wall.at[at], wy_s.at[d - 1], wy_r.at[d - 1], at_y(my_y + d))

    for d in range(1, ny):
        row_pieces(d).wait_recv()
    keys = dot(tok[...], wall[...].reshape(width, wide), NN)
    for m in range(mem):
        at = slice(m * hd, (m + 1) * hd)
        mk_h[:, at], mk_l[:, at] = split(column(1, m) * keys[:, at])
    mk2 = (mk_h[...], mk_l[...])
    ksend[...] = dot3(split(v_ref[...].T), mk2, NN).reshape(ksend.shape)
    each(1, nz, lambda d: scan_out(ksend, kin, ka_s, ka_r, d).start())
    kin[my_z] = ksend[my_z]

    each(1, nh, lambda d: token_share(d).wait_recv())
    for d in range(1, ny):
        tkt[:, d * count : (d + 1) * count] = tk[d - 1].T

    def key_rows(g, d):
        return copy(
            kgl.at[g], kgl_in.at[g, d - 1], ky_s.at[g, d - 1], ky_r.at[g, d - 1], at_y(my_y + d)
        )

    each(1, nz, lambda d: scan_out(gmid, gcar, gb_s, gb_r, d).wait_recv())
    gc_h[...], gc_l[...] = split(gcar[...].reshape(hd, wide))
    val2 = split(v_ref[...])
    for g in range(groups):
        at = slice(g * group_wide, (g + 1) * group_wide)
        carried_k = dot3(val2, (gc_h[:, at], gc_l[:, at]), NN) + inner[:, at]
        for i in range(group_wide // hd):
            m = g * (group_wide // hd) + i
            kgl[g, :, i * hd : (i + 1) * hd] = (
                column(1, m) * carried_k[:, i * hd : (i + 1) * hd]
            ).astype(BF16)
        for d in range(1, ny):
            key_rows(g, d).start()

    each(1, nz, lambda d: scan_out(ksend, kin, ka_s, ka_r, d).wait_recv())
    kback[...] = sweep(kin, kmid, False)
    for d in range(1, ny):
        scan_middle(kback, ktot, kt_s, kt_r, d).start()

    def flow(side, s, g):
        to = at_z(my_z + 1) if side == 0 else at_z(my_z - 1)
        return copy(
            stage.at[side, s - 1, g], land.at[side, s - 1, g],
            rs_s.at[side, s - 1, g], rs_r.at[side, s - 1, g], to,
        )

    def target(side, s):
        if side == 0:
            return lax.rem(my_z + right_hops + 1 - s, nz)
        return lax.rem(my_z - left_hops - 1 + s + 2 * nz, nz)

    def enter(g):
        for d in range(1, ny):
            key_rows(g, d).wait_recv()
        product = dot(tkt[:, 0:count], kgl[g], NN)
        for d in range(1, ny):
            product = product + dot(tkt[:, d * count : (d + 1) * count], kgl_in[g, d - 1], NN)
        prod[g] = product.reshape(prod.shape[1:])
        for side in range(2):
            stage[side, 0, g] = prod[g, target(side, 1)]
            flow(side, 1, g).start()

    enter(0)

    for d in range(1, ny):
        scan_middle(kback, ktot, kt_s, kt_r, d).wait_recv()
    extra = extra_of(ktot, False)
    for z in range(nz):
        whole = kmid[z] + extra
        kmid_low[z] = jnp.concatenate(
            [whole[:, 0 : wide // 2], whole[:, wide // 2 :]], axis=0
        ).astype(BF16)
    each(1, nz, lambda d: scan_out(kmid_low, kcar, kb_s, kb_r, d).start())
    kcar[my_z] = kmid_low[my_z]

    enter(1)

    def reduce_step(s):
        for g in range(groups):
            for side in range(2):
                flow(side, s - 1, g).wait_recv()
                stage[side, s - 1, g] = land[side, s - 2, g] + prod[g, target(side, s)]
                flow(side, s, g).start()

    early, later = min(2, right_hops), min(4, right_hops)
    for s in range(2, early + 1):
        reduce_step(s)

    dout2 = split(do_ref[...])
    mk2 = (mk_h[...], mk_l[...])
    mixed = jnp.where(places_t >= places_s, dot3(mk2, (lift_h[...], lift_l[...]), NT), 0.0)
    vg_out[...] = dot3(mk2, (gc_h[...], gc_l[...]), NT) + dot3(split(mixed), dout2, NN)

    for s in range(early + 1, later + 1):
        reduce_step(s)

    each(1, nz, lambda d: scan_out(kmid_low, kcar, kb_s, kb_r, d).wait_recv())
    rows = hd // nz
    carried = kcar[...]
    before = jnp.concatenate(
        [
            carried[:, 0:rows].reshape(hd, wide // 2),
            carried[:, rows : 2 * rows].reshape(hd, wide // 2),
        ],
        axis=1,
    )
    state = (
        dot(dout2[0], before, NN) + dot(dout2[1], before, NN)
        + dot3((sc_h[...], sc_l[...]), mk2, NN)
    )
    scaled_q = q_ref[...] * scale
    query = jnp.zeros((count, hd), F32)
    picks = [jnp.zeros((count, 1), F32), jnp.zeros((count, 1), F32)]
    for m in range(mem):
        here = state[:, m * hd : (m + 1) * hd]
        query = query + column(0, m) * here
        gradient = jnp.sum(scaled_q * here, axis=1, keepdims=True)
        for j in range(2):
            picks[j] = picks[j] + column(2 + j, m) * gradient
    qg_out[...] = scale * query
    lanes = lax.broadcasted_iota(jnp.int32, (count, hd), 1)
    spreaded = jnp.where(lanes == 0, picks[0], jnp.where(lanes == 1, picks[1], 0.0))
    gate[...] = spreaded.T[0:8, :]

    def gate_share(d):
        return copy(gate, gate_in.at[d - 1], gp_s.at[d - 1], gp_r.at[d - 1], at_head(head + d))

    each(1, nh, lambda d: gate_share(d).start())

    for s in range(later + 1, right_hops + 1):
        reduce_step(s)

    for g in range(groups):
        flow(1, left_hops - 1, g).wait_recv()
        stage[1, left_hops - 1, g] = land[1, left_hops - 2, g] + prod[g, target(1, left_hops)]
        flow(1, left_hops, g).start()

    each(1, nh, lambda d: gate_share(d).wait_recv())
    total = gate[...]
    for d in range(1, nh):
        total = total + gate_in[d - 1]
    gg_out[...] = total[0:2, :]

    for g in range(groups):
        flow(0, right_hops, g).wait_recv()
        flow(1, left_hops, g).wait_recv()
        done = prod[g, my_z] + land[0, right_hops - 1, g] + land[1, left_hops - 1, g]
        for i in range(group_wide // hd):
            kg_out[:, g * (group_wide // hd) + i, :] = done[:, i * hd : (i + 1) * hd]

    each(1, left_hops + 1, lambda k: ring_right(k).wait_send())
    each(1, right_hops + 1, lambda k: ring_left(k).wait_send())
    for d in range(1, ny):
        row_pieces(d).wait_send()
        token_rows(d).wait_send()
        scan_middle(gback, gtot, gt_s, gt_r, d).wait_send()
        scan_middle(kback, ktot, kt_s, kt_r, d).wait_send()
        for g in range(groups):
            key_rows(g, d).wait_send()

    def sent(d):
        scan_out(gsend, gin, ga_s, ga_r, d).wait_send()
        scan_out(gmid, gcar, gb_s, gb_r, d).wait_send()
        scan_out(ksend, kin, ka_s, ka_r, d).wait_send()
        scan_out(kmid_low, kcar, kb_s, kb_r, d).wait_send()

    each(1, nz, sent)

    def shared(d):
        token_share(d).wait_send()
        gate_share(d).wait_send()

    each(1, nh, shared)

    def reduced(s):
        for g in range(groups):
            flow(0, s, g).wait_send()
            flow(1, s, g).wait_send()

    each(1, right_hops + 1, reduced)
    for g in range(groups):
        flow(1, left_hops, g).wait_send()


def on_device(rows, tokens, queries, values, dout, key_weight, routing, gates):
    count, width = tokens.shape
    depth, mem, hd = key_weight.shape
    contexts, nh = lax.axis_size("ctx"), lax.axis_size("head")
    ny, nz = rows, contexts // rows
    wide = mem * hd
    scale = 1.0 / math.sqrt(hd * count * contexts)
    half = nz // 2
    dma = pltpu.SemaphoreType.DMA
    slab = (nz, hd // nz, wide)
    low_slab = (nz, 2 * (hd // nz), wide // 2)

    def scan(back):
        return [
            pltpu.VMEM(slab, F32),
            pltpu.VMEM(slab, F32),
            pltpu.VMEM(slab, F32),
            pltpu.VMEM((ny - 1,) + slab[1:], F32),
            pltpu.VMEM(slab[1:], F32),
            back,
        ]

    scan_sems = [dma((nz - 1,))] * 2 + [dma((ny - 1,))] * 2 + [dma((nz - 1,))] * 2
    scratch = (
        [
            pltpu.VMEM((count, width), BF16),
            pltpu.VMEM((count, hd), F32),
            pltpu.VMEM((count, hd), F32),
            pltpu.VMEM((count, hd), F32),
            pltpu.VMEM((depth, wide), BF16),
            pltpu.VMEM((2, count), jnp.int32),
            pltpu.VMEM((2, count), F32),
            dma((7,)),
            pltpu.VMEM((contexts, depth, wide), BF16),
            pltpu.VMEM((ny - 1, count, width // ny), BF16),
            pltpu.VMEM((width // ny, ny * count), BF16),
            pltpu.VMEM((2, count, wide // 2), BF16),
            pltpu.VMEM((2, ny - 1, count, wide // 2), BF16),
            pltpu.VMEM((count, wide), BF16),
            pltpu.VMEM((count, wide), BF16),
            pltpu.VMEM((count, wide), BF16),
            pltpu.VMEM((count, wide), BF16),
            pltpu.VMEM((count, 128), F32),
        ]
        + scan(pltpu.VMEM(slab, F32))
        + scan(pltpu.VMEM(low_slab, BF16))
        + [
            pltpu.VMEM(low_slab, BF16),
            pltpu.VMEM((2, nz, depth, wide // 2), F32),
            pltpu.VMEM((2, half, 2, depth, wide // 2), F32),
            pltpu.VMEM((2, half, 2, depth, wide // 2), F32),
            pltpu.VMEM((8, count), F32),
            pltpu.VMEM((nh - 1, 8, count), F32),
            pltpu.VMEM((count, count), BF16),
            pltpu.VMEM((count, count), BF16),
            pltpu.VMEM((count, wide), F32),
            pltpu.VMEM((hd, wide), BF16),
            pltpu.VMEM((hd, wide), BF16),
        ]
        + [dma((2, half))] * 2
        + [dma((ny - 1,))] * 4
        + [dma((nh - 1,))] * 2
        + scan_sems
        + scan_sems
        + [dma((2, ny - 1))] * 2
        + [dma((2, half, 2))] * 2
        + [dma((nh - 1,))] * 2
    )
    vmem = pl.BlockSpec(memory_space=pltpu.VMEM)
    anywhere = pl.BlockSpec(memory_space=pl.ANY)
    key_grad, query_grad, value_grad, gate_grad = pl.pallas_call(
        functools.partial(kernel, (ny, nz, nh, mem, hd, scale)),
        out_shape=(
            jax.ShapeDtypeStruct((depth, mem, hd), F32),
            jax.ShapeDtypeStruct((count, hd), F32),
            jax.ShapeDtypeStruct((count, hd), F32),
            jax.ShapeDtypeStruct((2, count), F32),
        ),
        in_specs=[anywhere] * 7,
        out_specs=(vmem,) * 4,
        scratch_shapes=scratch,
        compiler_params=pltpu.CompilerParams(
            collective_id=0, has_side_effects=True, vmem_limit_bytes=56 * 1024 * 1024
        ),
    )(tokens, queries, values, dout, key_weight.reshape(depth, wide), routing.T, gates.T)
    return key_grad, query_grad, value_grad, gate_grad.T


def solution(mesh, rows=4):
    return jax.shard_map(
        functools.partial(on_device, rows),
        mesh=mesh,
        in_specs=(
            P("ctx", None),
            P("ctx", "head"),
            P("ctx", "head"),
            P("ctx", "head"),
            P("ctx", None, "head"),
            P("ctx", None),
            P("ctx", None),
        ),
        out_specs=(P("ctx", None, "head"), P("ctx", "head"), P("ctx", "head"), P("ctx", None)),
        check_vma=False,
    )
```

```python
import functools
import math

import jax
import jax.numpy as jnp
from jax import lax
from jax.experimental import pallas as pl
from jax.experimental.pallas import tpu as pltpu
from jax.sharding import PartitionSpec as P

MESH = pl.DeviceIdType.MESH
F32 = jnp.float32
BF16 = jnp.bfloat16
NN = (((1,), (0,)), ((), ()))
NT = (((1,), (1,)), ((), ()))


def split(x):
    high = x.astype(BF16)
    return high, (x - high.astype(F32)).astype(BF16)


def dot(a, b, dims):
    return lax.dot_general(a, b, dims, preferred_element_type=F32)


def dot3(a, b, dims):
    return dot(a[0], b[0], dims) + (dot(a[0], b[1], dims) + dot(a[1], b[0], dims))


def each(lower, upper, body):
    def step(i, carry):
        body(i)
        return carry

    lax.fori_loop(lower, upper, step, 0)


def runs_of(nz):
    near, far = nz // 2 // 2, nz // 2 - nz // 2 // 2
    short = (nz // 2 - 1 + 1) // 2
    spread = [(1, 0, near), (1, near, far), (-1, 0, short), (-1, short, nz // 2 - 1 - short)]
    low = (nz // 2 - 1) // 2
    reduce = [(1, 0, low), (1, low, nz // 2 - 1 - low), (-1, 0, near), (-1, near, far)]
    return [r for r in spread if r[2]], [r for r in reduce if r[2]]


def kernel(
    sizes,
    tok_hbm, q_hbm, v_hbm, do_hbm, w_hbm, r_hbm, g_hbm,
    kg_out, qg_out, vg_out, gg_out,
    tok, q_ref, v_ref, do_ref, w_ref, r_ref, g_ref, in_sems,
    wall, tk, tkt, kgl, kgl_in, lift_h, lift_l, mk_h, mk_l, cols,
    gsend, gin, gmid, gtot, gback, gcar, gmid_low,
    ksend, kin, kmid, ktot, kback, kcar, kmid_low,
    prod, stage, land, gate, gate_in,
    sc_h, sc_l, inner, gc,
    ww_s, ww_r, wy_s, wy_r, ty_s, ty_r, th_s, th_r,
    ga_s, ga_r, gt_s, gt_r, gb_s, gb_r,
    ka_s, ka_r, kt_s, kt_r, kb_s, kb_r,
    ky_s, ky_r, rs_s, rs_r, gp_s, gp_r,
):
    ny, nz, nh, mem, hd, scale = sizes
    ctx, head = lax.axis_index("ctx"), lax.axis_index("head")
    my_y, my_z = ctx // nz, ctx % nz
    count, width = tok.shape
    wide = mem * hd
    part = count // nh
    lane = width // ny
    groups = 2
    group_wide = wide // groups
    spread_runs, reduce_runs = runs_of(nz)
    longest = max(n for _, _, n in spread_runs)
    reduce_longest = max(n for _, _, n in reduce_runs)

    def at_z(z):
        return {"ctx": my_y * nz + lax.rem(z + 2 * nz, nz)}

    def at_y(y):
        return {"ctx": lax.rem(y + ny, ny) * nz + my_z}

    def at_head(h):
        return {"head": lax.rem(h, nh)}

    def copy(src, dst, send, recv, to):
        return pltpu.make_async_remote_copy(
            src_ref=src, dst_ref=dst, send_sem=send, recv_sem=recv,
            device_id=to, device_id_type=MESH,
        )

    barrier = pltpu.get_barrier_semaphore()

    def greet(to):
        pl.semaphore_signal(barrier, inc=1, device_id=to, device_id_type=MESH)

    each(1, nz, lambda d: greet(at_z(my_z + d)))
    each(1, ny, lambda d: greet(at_y(my_y + d)))
    each(1, nh, lambda d: greet(at_head(head + d)))

    fetches = [
        pltpu.make_async_copy(src, dst, in_sems.at[i])
        for i, (src, dst) in enumerate(
            [
                (r_hbm, r_ref), (g_hbm, g_ref), (q_hbm, q_ref), (do_hbm, do_ref),
                (v_hbm, v_ref), (w_hbm, w_ref), (tok_hbm, tok),
            ]
        )
    ]
    for fetch in fetches:
        fetch.start()
    for fetch in fetches[:4]:
        fetch.wait()

    row = lax.broadcasted_iota(jnp.int32, (128, count), 0)
    memory, group = row % mem, row // mem
    first = (r_ref[0:1, :] == memory).astype(F32)
    second = (r_ref[1:2, :] == memory).astype(F32)
    weights = g_ref[0:1, :] * first + g_ref[1:2, :] * second
    table = jnp.where(
        group == 0, weights,
        jnp.where(group == 1, first + second, jnp.where(group == 2, first, jnp.where(group == 3, second, 0.0))),
    )
    cols[...] = table.T

    def column(kind, m):
        return cols[:, kind * mem + m : kind * mem + m + 1]

    scaled_q = q_ref[...] * scale
    for m in range(mem):
        high, low = split(column(0, m) * scaled_q)
        lift_h[:, m * hd : (m + 1) * hd] = high
        lift_l[:, m * hd : (m + 1) * hd] = low

    local = dot3(split(do_ref[...].T), (lift_h[...], lift_l[...]), NN)
    for g in range(groups):
        gsend[g] = local[:, g * group_wide : (g + 1) * group_wide].reshape(gsend.shape[1:])

    fetches[4].wait()
    fetches[5].wait()
    places_s = lax.broadcasted_iota(jnp.int32, (count, count), 0)
    places_t = lax.broadcasted_iota(jnp.int32, (count, count), 1)
    dout2 = split(do_ref[...])
    val2 = split(v_ref[...])
    scores = jnp.where(places_s >= places_t, dot3(dout2, val2, NT), 0.0)
    sc_h[...], sc_l[...] = split(scores)
    scores_t = split(jnp.where(places_t >= places_s, dot3(val2, dout2, NT), 0.0))
    inner[...] = dot3(scores_t, (lift_h[...], lift_l[...]), NN)
    fetches[6].wait()
    own_lanes = pl.ds(pl.multiple_of(my_y * lane, lane), lane)
    tkt[:, 0:count] = tok[:, own_lanes].T

    pl.semaphore_wait(barrier, (nz - 1) + (ny - 1) + (nh - 1))

    def hop(run, k, src=None):
        side, base, _ = spread_runs[run]
        at = my_y * nz + lax.rem(my_z - side * (base + k - 1 if k > 1 else 0) + nz, nz)
        src = wall.at[at] if src is None else src
        to = at_z(my_z + side * (1 if k > 1 else base + 1))
        return copy(src, wall.at[at], ww_s.at[run, k - 1], ww_r.at[run, k - 1], to)

    def to_rows(z, src=None):
        at = my_y * nz + lax.rem(z + 2 * nz, nz)
        for d in range(1, ny):
            copy(
                wall.at[at] if src is None else src, wall.at[at],
                wy_s.at[d - 1], wy_r.at[d - 1], at_y(my_y + d),
            ).start()

    def scan_out(src, dst, send, recv, d):
        z = lax.rem(my_z + d, nz)
        return copy(src.at[z], dst.at[my_z], send.at[d - 1], recv.at[d - 1], at_z(z))

    for run in range(len(spread_runs)):
        hop(run, 1, w_ref).start()

    def first_out(g, d):
        return scan_out(gsend.at[g], gin.at[g], ga_s.at[g], ga_r.at[g], d)

    def first_back(g, d):
        return scan_out(gmid_low.at[g], gcar.at[g], gb_s.at[g], gb_r.at[g], d)

    each(1, nz, lambda d: first_out(0, d).start())

    def token_rows(d):
        y = lax.rem(my_y + d, ny)
        rows = pl.ds(pl.multiple_of(head * part, part), part)
        return copy(
            tok.at[rows, pl.ds(pl.multiple_of(y * lane, lane), lane)],
            tk.at[d - 1, rows], ty_s.at[d - 1], ty_r.at[d - 1], at_y(y),
        )

    for d in range(1, ny):
        token_rows(d).start()
    to_rows(my_z, w_ref)
    wall[ctx] = w_ref[...]
    for g in range(groups):
        gin[g, my_z] = gsend[g, my_z]

    def ring_step(k):
        here = [run for run in range(len(spread_runs)) if k <= spread_runs[run][2]]
        for run in here:
            hop(run, k).wait_recv()
            if k < spread_runs[run][2]:
                hop(run, k + 1).start()
        for run in here:
            side, base, _ = spread_runs[run]
            to_rows(my_z - side * (base + k))

    def scan_middle(src, tot, send, recv, d):
        return copy(src, tot.at[d - 1], send.at[d - 1], recv.at[d - 1], at_y(my_y + d))

    def first_middle(g, d):
        return scan_middle(gback.at[g], gtot.at[g], gt_s.at[g], gt_r.at[g], d)

    def sweep(inbox, mid, backwards):
        total = jnp.zeros(inbox.shape[1:], F32)
        for z in reversed(range(nz)) if backwards else range(nz):
            mid[z] = total
            total = total + inbox[z].astype(F32)
        return total

    def extra_of(tot, backwards):
        extra = jnp.zeros(tot.shape[1:], F32)
        for d in range(1, ny):
            y = lax.rem(my_y - d + ny, ny)
            reached = (y > my_y) if backwards else (y < my_y)
            extra = extra + tot[d - 1] * reached.astype(F32)
        return extra

    def totals(g):
        each(1, nz, lambda d: first_out(g, d).wait_recv())
        gback[g] = sweep(gin.at[g], gmid.at[g], True)
        for d in range(1, ny):
            first_middle(g, d).start()

    def send_back(g):
        for d in range(1, ny):
            first_middle(g, d).wait_recv()
        extra = extra_of(gtot.at[g], True)
        for z in range(nz):
            whole = gmid[g, z] + extra
            gmid_low[g, z] = jnp.concatenate(
                [whole[:, 0 : group_wide // 2], whole[:, group_wide // 2 :]], axis=0
            ).astype(BF16)
        each(1, nz, lambda d: first_back(g, d).start())
        gcar[g, my_z] = gmid_low[g, my_z]

    def token_share(d):
        rows = pl.ds(pl.multiple_of(head * part, part), part)
        return copy(tk.at[:, rows], tk.at[:, rows], th_s.at[d - 1], th_r.at[d - 1], at_head(head + d))

    for k in range(1, min(2, longest) + 1):
        ring_step(k)
    each(1, nz, lambda d: first_out(1, d).start())
    totals(0)
    if longest > 2:
        ring_step(3)
    for d in range(1, ny):
        token_rows(d).wait_recv()
    each(1, nh, lambda d: token_share(d).start())
    send_back(0)
    for k in range(4, longest + 1):
        ring_step(k)
    totals(1)
    send_back(1)

    def key_rows(g, d):
        return copy(
            kgl.at[g], kgl_in.at[g, d - 1], ky_s.at[g, d - 1], ky_r.at[g, d - 1], at_y(my_y + d)
        )

    def unfold(slabs, rows):
        half = slabs.shape[2]
        return jnp.concatenate(
            [slabs[:, 0:rows].reshape(hd, half), slabs[:, rows : 2 * rows].reshape(hd, half)], axis=1
        )

    slice_rows = hd // nz

    def own_keys(g):
        each(1, nz, lambda d: first_back(g, d).wait_recv())
        at = slice(g * group_wide, (g + 1) * group_wide)
        before = unfold(gcar[g], slice_rows)
        gc[g] = before
        high, low = split(v_ref[...])
        carried_k = dot(high, before, NN) + dot(low, before, NN) + inner[:, at]
        for i in range(group_wide // hd):
            m = g * (group_wide // hd) + i
            kgl[g, :, i * hd : (i + 1) * hd] = (
                column(1, m) * carried_k[:, i * hd : (i + 1) * hd]
            ).astype(BF16)
        for d in range(1, ny):
            key_rows(g, d).start()

    own_keys(0)
    each(1, nh, lambda d: token_share(d).wait_recv())
    for d in range(1, ny):
        tkt[:, d * count : (d + 1) * count] = tk[d - 1].T
    own_keys(1)

    def row_pieces(d):
        y = lax.rem(my_y - d + ny, ny)
        at = pl.ds(y * nz, nz)
        return copy(wall.at[at], wall.at[at], wy_s.at[d - 1], wy_r.at[d - 1], at_y(my_y + d))

    for d in range(1, ny):
        row_pieces(d).wait_recv()
    keys = dot(tok[...], wall[...].reshape(width, wide), NN)
    for m in range(mem):
        at = slice(m * hd, (m + 1) * hd)
        mk_h[:, at], mk_l[:, at] = split(column(1, m) * keys[:, at])
    mk2 = (mk_h[...], mk_l[...])
    local = dot3(split(v_ref[...].T), mk2, NN)
    ksend[...] = jnp.concatenate(
        [
            local[:, 0 : wide // 2].reshape(nz, slice_rows, wide // 2),
            local[:, wide // 2 :].reshape(nz, slice_rows, wide // 2),
        ],
        axis=1,
    ).astype(BF16)

    def second_out(d):
        return scan_out(ksend, kin, ka_s, ka_r, d)

    def second_back(d):
        return scan_out(kmid_low, kcar, kb_s, kb_r, d)

    def second_middle(d):
        return scan_middle(kback, ktot, kt_s, kt_r, d)

    each(1, nz, lambda d: second_out(d).start())
    kin[my_z] = ksend[my_z]

    def flow(run, s, g):
        side, base, hops = reduce_runs[run]
        to = at_z(my_z + side * (1 if s < hops else base + 1))
        return copy(
            stage.at[run, s - 1, g], land.at[run, s - 1, g],
            rs_s.at[run, s - 1, g], rs_r.at[run, s - 1, g], to,
        )

    def target(run, s):
        side, base, hops = reduce_runs[run]
        return lax.rem(my_z + side * (base + hops - s + 1) + nz, nz)

    def enter(g):
        for d in range(1, ny):
            key_rows(g, d).wait_recv()
        product = dot(tkt[:, 0:count], kgl[g], NN)
        for d in range(1, ny):
            product = product + dot(tkt[:, d * count : (d + 1) * count], kgl_in[g, d - 1], NN)
        prod[g] = product.reshape(prod.shape[1:])
        for run in range(len(reduce_runs)):
            stage[run, 0, g] = prod[g, target(run, 1)]
            flow(run, 1, g).start()

    def reduce_step(g, s):
        for run in range(len(reduce_runs)):
            if s <= reduce_runs[run][2]:
                flow(run, s - 1, g).wait_recv()
                stage[run, s - 1, g] = land[run, s - 2, g] + prod[g, target(run, s)]
                flow(run, s, g).start()

    def reduce_end(g):
        done = prod[g, my_z]
        for run in range(len(reduce_runs)):
            hops = reduce_runs[run][2]
            flow(run, hops, g).wait_recv()
            done = done + land[run, hops - 1, g]
        for i in range(group_wide // hd):
            kg_out[:, g * (group_wide // hd) + i, :] = done[:, i * hd : (i + 1) * hd]

    def second_totals():
        each(1, nz, lambda d: second_out(d).wait_recv())
        kback[...] = sweep(kin, kmid, False)
        for d in range(1, ny):
            second_middle(d).start()

    def second_send_back():
        for d in range(1, ny):
            second_middle(d).wait_recv()
        extra = extra_of(ktot, False)
        for z in range(nz):
            kmid_low[z] = (kmid[z] + extra).astype(BF16)
        each(1, nz, lambda d: second_back(d).start())
        kcar[my_z] = kmid_low[my_z]

    def value_part():
        dout2 = split(do_ref[...])
        mk2 = (mk_h[...], mk_l[...])
        mixed = jnp.where(places_t >= places_s, dot3(mk2, (lift_h[...], lift_l[...]), NT), 0.0)
        total = dot3(split(mixed), dout2, NN)
        for g in range(groups):
            at = slice(g * group_wide, (g + 1) * group_wide)
            total = total + dot(mk2[0][:, at], gc[g], NT) + dot(mk2[1][:, at], gc[g], NT)
        vg_out[...] = total

    def gate_share(d):
        return copy(gate, gate_in.at[d - 1], gp_s.at[d - 1], gp_r.at[d - 1], at_head(head + d))

    def query_part():
        each(1, nz, lambda d: second_back(d).wait_recv())
        dout2 = split(do_ref[...])
        before = unfold(kcar[...], slice_rows)
        state = (
            dot(dout2[0], before, NN) + dot(dout2[1], before, NN)
            + dot3((sc_h[...], sc_l[...]), (mk_h[...], mk_l[...]), NN)
        )
        scaled_q = q_ref[...] * scale
        query = jnp.zeros((count, hd), F32)
        picks = [jnp.zeros((count, 1), F32), jnp.zeros((count, 1), F32)]
        for m in range(mem):
            here = state[:, m * hd : (m + 1) * hd]
            query = query + column(0, m) * here
            gradient = jnp.sum(scaled_q * here, axis=1, keepdims=True)
            for j in range(2):
                picks[j] = picks[j] + column(2 + j, m) * gradient
        qg_out[...] = scale * query
        lanes = lax.broadcasted_iota(jnp.int32, (count, hd), 1)
        spreaded = jnp.where(lanes == 0, picks[0], jnp.where(lanes == 1, picks[1], 0.0))
        gate[...] = spreaded.T[0:8, :]
        each(1, nh, lambda d: gate_share(d).start())

    def reduce_from(g, lower, upper):
        for s in range(lower, min(upper, reduce_longest) + 1):
            reduce_step(g, s)

    enter(0)
    reduce_from(0, 2, 2)
    enter(1)
    second_totals()
    reduce_from(0, 3, 3)
    reduce_from(1, 2, 2)
    second_send_back()
    reduce_from(0, 4, reduce_longest)
    reduce_from(1, 3, reduce_longest)
    value_part()
    query_part()
    for g in range(groups):
        reduce_end(g)

    each(1, nh, lambda d: gate_share(d).wait_recv())
    total = gate[...]
    for d in range(1, nh):
        total = total + gate_in[d - 1]
    gg_out[...] = total[0:2, :]

    for run, (_, _, hops) in enumerate(spread_runs):
        for k in range(1, hops + 1):
            hop(run, k).wait_send()
    for run, (_, _, hops) in enumerate(reduce_runs):
        for s in range(1, hops + 1):
            for g in range(groups):
                flow(run, s, g).wait_send()
    for d in range(1, ny):
        row_pieces(d).wait_send()
        token_rows(d).wait_send()
        second_middle(d).wait_send()
        for g in range(groups):
            first_middle(g, d).wait_send()
            key_rows(g, d).wait_send()

    def sent(d):
        second_out(d).wait_send()
        second_back(d).wait_send()
        for g in range(groups):
            first_out(g, d).wait_send()
            first_back(g, d).wait_send()

    each(1, nz, sent)

    def shared(d):
        token_share(d).wait_send()
        gate_share(d).wait_send()

    each(1, nh, shared)


def on_device(rows, tokens, queries, values, dout, key_weight, routing, gates):
    count, width = tokens.shape
    depth, mem, hd = key_weight.shape
    contexts, nh = lax.axis_size("ctx"), lax.axis_size("head")
    ny, nz = rows, contexts // rows
    wide = mem * hd
    scale = 1.0 / math.sqrt(hd * count * contexts)
    half = nz // 2
    dma = pltpu.SemaphoreType.DMA
    rows_z = hd // nz
    slab = (2, nz, rows_z, wide // 2)
    low_slab = (2, nz, 2 * rows_z, wide // 4)
    fold = (nz, 2 * rows_z, wide // 2)
    first_scan = [
        pltpu.VMEM(slab, F32),
        pltpu.VMEM(slab, F32),
        pltpu.VMEM(slab, F32),
        pltpu.VMEM((2, ny - 1) + slab[2:], F32),
        pltpu.VMEM((2,) + slab[2:], F32),
        pltpu.VMEM(low_slab, BF16),
        pltpu.VMEM(low_slab, BF16),
    ]
    second_scan = [
        pltpu.VMEM(fold, BF16),
        pltpu.VMEM(fold, BF16),
        pltpu.VMEM(fold, F32),
        pltpu.VMEM((ny - 1,) + fold[1:], F32),
        pltpu.VMEM(fold[1:], F32),
        pltpu.VMEM(fold, BF16),
        pltpu.VMEM(fold, BF16),
    ]
    first_sems = [dma((2, nz - 1))] * 2 + [dma((2, ny - 1))] * 2 + [dma((2, nz - 1))] * 2
    second_sems = [dma((nz - 1,))] * 2 + [dma((ny - 1,))] * 2 + [dma((nz - 1,))] * 2
    scratch = (
        [
            pltpu.VMEM((count, width), BF16),
            pltpu.VMEM((count, hd), F32),
            pltpu.VMEM((count, hd), F32),
            pltpu.VMEM((count, hd), F32),
            pltpu.VMEM((depth, wide), BF16),
            pltpu.VMEM((2, count), jnp.int32),
            pltpu.VMEM((2, count), F32),
            dma((7,)),
            pltpu.VMEM((contexts, depth, wide), BF16),
            pltpu.VMEM((ny - 1, count, width // ny), BF16),
            pltpu.VMEM((width // ny, ny * count), BF16),
            pltpu.VMEM((2, count, wide // 2), BF16),
            pltpu.VMEM((2, ny - 1, count, wide // 2), BF16),
            pltpu.VMEM((count, wide), BF16),
            pltpu.VMEM((count, wide), BF16),
            pltpu.VMEM((count, wide), BF16),
            pltpu.VMEM((count, wide), BF16),
            pltpu.VMEM((count, 128), F32),
        ]
        + first_scan
        + second_scan
        + [
            pltpu.VMEM((2, nz, depth, wide // 2), F32),
            pltpu.VMEM((4, half, 2, depth, wide // 2), F32),
            pltpu.VMEM((4, half, 2, depth, wide // 2), F32),
            pltpu.VMEM((8, count), F32),
            pltpu.VMEM((nh - 1, 8, count), F32),
            pltpu.VMEM((count, count), BF16),
            pltpu.VMEM((count, count), BF16),
            pltpu.VMEM((count, wide), F32),
            pltpu.VMEM((2, hd, wide // 2), BF16),
        ]
        + [dma((4, half))] * 2
        + [dma((ny - 1,))] * 4
        + [dma((nh - 1,))] * 2
        + first_sems
        + second_sems
        + [dma((2, ny - 1))] * 2
        + [dma((4, half, 2))] * 2
        + [dma((nh - 1,))] * 2
    )
    vmem = pl.BlockSpec(memory_space=pltpu.VMEM)
    anywhere = pl.BlockSpec(memory_space=pl.ANY)
    key_grad, query_grad, value_grad, gate_grad = pl.pallas_call(
        functools.partial(kernel, (ny, nz, nh, mem, hd, scale)),
        out_shape=(
            jax.ShapeDtypeStruct((depth, mem, hd), F32),
            jax.ShapeDtypeStruct((count, hd), F32),
            jax.ShapeDtypeStruct((count, hd), F32),
            jax.ShapeDtypeStruct((2, count), F32),
        ),
        in_specs=[anywhere] * 7,
        out_specs=(vmem,) * 4,
        scratch_shapes=scratch,
        compiler_params=pltpu.CompilerParams(
            collective_id=0, has_side_effects=True, vmem_limit_bytes=56 * 1024 * 1024
        ),
    )(tokens, queries, values, dout, key_weight.reshape(depth, wide), routing.T, gates.T)
    return key_grad, query_grad, value_grad, gate_grad.T


def solution(mesh, rows=4):
    return jax.shard_map(
        functools.partial(on_device, rows),
        mesh=mesh,
        in_specs=(
            P("ctx", None),
            P("ctx", "head"),
            P("ctx", "head"),
            P("ctx", "head"),
            P("ctx", None, "head"),
            P("ctx", None),
            P("ctx", None),
        ),
        out_specs=(P("ctx", None, "head"), P("ctx", "head"), P("ctx", "head"), P("ctx", None)),
        check_vma=False,
    )
```

```python
import functools
import math

import jax
import jax.numpy as jnp
from jax import lax
from jax.experimental import pallas as pl
from jax.experimental.pallas import tpu as pltpu
from jax.sharding import PartitionSpec as P

MESH = pl.DeviceIdType.MESH
F32 = jnp.float32
BF16 = jnp.bfloat16
NN = (((1,), (0,)), ((), ()))
NT = (((1,), (1,)), ((), ()))


def split(x):
    high = x.astype(BF16)
    return high, (x - high.astype(F32)).astype(BF16)


def dot(a, b, dims):
    return lax.dot_general(a, b, dims, preferred_element_type=F32)


def dot3(a, b, dims):
    return dot(a[0], b[0], dims) + (dot(a[0], b[1], dims) + dot(a[1], b[0], dims))


def each(lower, upper, body):
    def step(i, carry):
        body(i)
        return carry

    lax.fori_loop(lower, upper, step, 0)


def runs_of(nz):
    near, far = nz // 2 // 2, nz // 2 - nz // 2 // 2
    short = (nz // 2 - 1 + 1) // 2
    spread = [(1, 0, near), (1, near, far), (-1, 0, short), (-1, short, nz // 2 - 1 - short)]
    low = (nz // 2 - 1) // 2
    reduce = [(1, 0, low), (1, low, nz // 2 - 1 - low), (-1, 0, near), (-1, near, far)]
    return [r for r in spread if r[2]], [r for r in reduce if r[2]]


def kernel(
    sizes,
    tok_hbm, q_hbm, v_hbm, do_hbm, w_hbm, r_hbm, g_hbm,
    kg_out, qg_out, vg_out, gg_out,
    tok, q_ref, v_ref, do_ref, w_cut, w_ref, r_ref, g_ref, in_sems,
    wall, tk, tkt, kgl, kgl_in, lift_h, lift_l, mk_h, mk_l, cols,
    gsend, gin, gmid, gtot, gback, gcar, gmid_low,
    ksend, kin, kmid, ktot, kback, kcar, kmid_low,
    prod, stage, land, gate, gate_in,
    sc_h, sc_l, inner, gc,
    ww_s, ww_r, wy_s, wy_r, ty_s, ty_r, th_s, th_r,
    ga_s, ga_r, gt_s, gt_r, gb_s, gb_r,
    ka_s, ka_r, kt_s, kt_r, kb_s, kb_r,
    ky_s, ky_r, rs_s, rs_r, gp_s, gp_r,
):
    ny, nz, nh, mem, hd, scale = sizes
    ctx, head = lax.axis_index("ctx"), lax.axis_index("head")
    my_y, my_z = ctx // nz, ctx % nz
    count, width = tok.shape
    wide = mem * hd
    part = count // nh
    lane = width // ny
    groups = 2
    group_wide = wide // groups
    spread_runs, reduce_runs = runs_of(nz)
    longest = max(n for _, _, n in spread_runs)
    reduce_longest = max(n for _, _, n in reduce_runs)

    def at_z(z):
        return {"ctx": my_y * nz + lax.rem(z + 2 * nz, nz)}

    def at_y(y):
        return {"ctx": lax.rem(y + ny, ny) * nz + my_z}

    def at_head(h):
        return {"head": lax.rem(h, nh)}

    def copy(src, dst, send, recv, to):
        return pltpu.make_async_remote_copy(
            src_ref=src, dst_ref=dst, send_sem=send, recv_sem=recv,
            device_id=to, device_id_type=MESH,
        )

    barrier = pltpu.get_barrier_semaphore()

    def greet(to):
        pl.semaphore_signal(barrier, inc=1, device_id=to, device_id_type=MESH)

    each(1, nz, lambda d: greet(at_z(my_z + d)))
    each(1, ny, lambda d: greet(at_y(my_y + d)))
    each(1, nh, lambda d: greet(at_head(head + d)))

    fetches = [
        pltpu.make_async_copy(src, dst, in_sems.at[i])
        for i, (src, dst) in enumerate(
            [
                (r_hbm, r_ref), (g_hbm, g_ref), (q_hbm, q_ref), (do_hbm, do_ref),
                (v_hbm, v_ref), (w_hbm, w_cut), (tok_hbm, tok),
            ]
        )
    ]
    for fetch in fetches:
        fetch.start()
    for fetch in fetches[:4]:
        fetch.wait()

    row = lax.broadcasted_iota(jnp.int32, (128, count), 0)
    memory, group = row % mem, row // mem
    first = (r_ref[0:1, :] == memory).astype(F32)
    second = (r_ref[1:2, :] == memory).astype(F32)
    weights = g_ref[0:1, :] * first + g_ref[1:2, :] * second
    table = jnp.where(
        group == 0, weights,
        jnp.where(group == 1, first + second, jnp.where(group == 2, first, jnp.where(group == 3, second, 0.0))),
    )
    cols[...] = table.T

    def column(kind, m):
        return cols[:, kind * mem + m : kind * mem + m + 1]

    scaled_q = q_ref[...] * scale
    for m in range(mem):
        high, low = split(column(0, m) * scaled_q)
        lift_h[:, m * hd : (m + 1) * hd] = high
        lift_l[:, m * hd : (m + 1) * hd] = low

    local = dot3(split(do_ref[...].T), (lift_h[...], lift_l[...]), NN)
    for g in range(groups):
        gsend[g] = local[:, g * group_wide : (g + 1) * group_wide].reshape(gsend.shape[1:])

    fetches[4].wait()
    fetches[5].wait()
    for m in range(mem):
        w_ref[:, m * hd : (m + 1) * hd] = w_cut[:, m, :]
    places_s = lax.broadcasted_iota(jnp.int32, (count, count), 0)
    places_t = lax.broadcasted_iota(jnp.int32, (count, count), 1)
    dout2 = split(do_ref[...])
    val2 = split(v_ref[...])
    scores = jnp.where(places_s >= places_t, dot3(dout2, val2, NT), 0.0)
    sc_h[...], sc_l[...] = split(scores)
    scores_t = split(jnp.where(places_t >= places_s, dot3(val2, dout2, NT), 0.0))
    inner[...] = dot3(scores_t, (lift_h[...], lift_l[...]), NN)
    fetches[6].wait()
    own_lanes = pl.ds(pl.multiple_of(my_y * lane, lane), lane)
    tkt[:, 0:count] = tok[:, own_lanes].T

    pl.semaphore_wait(barrier, (nz - 1) + (ny - 1) + (nh - 1))

    def hop(run, k, src=None):
        side, base, _ = spread_runs[run]
        at = my_y * nz + lax.rem(my_z - side * (base + k - 1 if k > 1 else 0) + nz, nz)
        src = wall.at[at] if src is None else src
        to = at_z(my_z + side * (1 if k > 1 else base + 1))
        return copy(src, wall.at[at], ww_s.at[run, k - 1], ww_r.at[run, k - 1], to)

    def to_rows(z, src=None):
        at = my_y * nz + lax.rem(z + 2 * nz, nz)
        for d in range(1, ny):
            copy(
                wall.at[at] if src is None else src, wall.at[at],
                wy_s.at[d - 1], wy_r.at[d - 1], at_y(my_y + d),
            ).start()

    def scan_out(src, dst, send, recv, d):
        z = lax.rem(my_z + d, nz)
        return copy(src.at[z], dst.at[my_z], send.at[d - 1], recv.at[d - 1], at_z(z))

    for run in range(len(spread_runs)):
        hop(run, 1, w_ref).start()

    def first_out(g, d):
        return scan_out(gsend.at[g], gin.at[g], ga_s.at[g], ga_r.at[g], d)

    def first_back(g, d):
        return scan_out(gmid_low.at[g], gcar.at[g], gb_s.at[g], gb_r.at[g], d)

    each(1, nz, lambda d: first_out(0, d).start())

    def token_rows(d):
        y = lax.rem(my_y + d, ny)
        rows = pl.ds(pl.multiple_of(head * part, part), part)
        return copy(
            tok.at[rows, pl.ds(pl.multiple_of(y * lane, lane), lane)],
            tk.at[d - 1, rows], ty_s.at[d - 1], ty_r.at[d - 1], at_y(y),
        )

    for d in range(1, ny):
        token_rows(d).start()
    to_rows(my_z, w_ref)
    wall[ctx] = w_ref[...]
    for g in range(groups):
        gin[g, my_z] = gsend[g, my_z]

    def ring_step(k):
        here = [run for run in range(len(spread_runs)) if k <= spread_runs[run][2]]
        for run in here:
            hop(run, k).wait_recv()
            if k < spread_runs[run][2]:
                hop(run, k + 1).start()
        for run in here:
            side, base, _ = spread_runs[run]
            to_rows(my_z - side * (base + k))

    def scan_middle(src, tot, send, recv, d):
        return copy(src, tot.at[d - 1], send.at[d - 1], recv.at[d - 1], at_y(my_y + d))

    def first_middle(g, d):
        return scan_middle(gback.at[g], gtot.at[g], gt_s.at[g], gt_r.at[g], d)

    def sweep(inbox, mid, backwards):
        total = jnp.zeros(inbox.shape[1:], F32)
        for z in reversed(range(nz)) if backwards else range(nz):
            mid[z] = total
            total = total + inbox[z].astype(F32)
        return total

    def extra_of(tot, backwards):
        extra = jnp.zeros(tot.shape[1:], F32)
        for d in range(1, ny):
            y = lax.rem(my_y - d + ny, ny)
            reached = (y > my_y) if backwards else (y < my_y)
            extra = extra + tot[d - 1] * reached.astype(F32)
        return extra

    def totals(g):
        each(1, nz, lambda d: first_out(g, d).wait_recv())
        gback[g] = sweep(gin.at[g], gmid.at[g], True)
        for d in range(1, ny):
            first_middle(g, d).start()

    def send_back(g):
        for d in range(1, ny):
            first_middle(g, d).wait_recv()
        extra = extra_of(gtot.at[g], True)
        for z in range(nz):
            whole = gmid[g, z] + extra
            gmid_low[g, z] = jnp.concatenate(
                [whole[:, 0 : group_wide // 2], whole[:, group_wide // 2 :]], axis=0
            ).astype(BF16)
        each(1, nz, lambda d: first_back(g, d).start())
        gcar[g, my_z] = gmid_low[g, my_z]

    def token_share(d):
        rows = pl.ds(pl.multiple_of(head * part, part), part)
        return copy(tk.at[:, rows], tk.at[:, rows], th_s.at[d - 1], th_r.at[d - 1], at_head(head + d))

    for k in range(1, min(2, longest) + 1):
        ring_step(k)
    each(1, nz, lambda d: first_out(1, d).start())
    totals(0)
    if longest > 2:
        ring_step(3)
    for d in range(1, ny):
        token_rows(d).wait_recv()
    each(1, nh, lambda d: token_share(d).start())
    send_back(0)
    for k in range(4, longest + 1):
        ring_step(k)
    totals(1)
    send_back(1)

    def key_rows(g, d):
        return copy(
            kgl.at[g], kgl_in.at[g, d - 1], ky_s.at[g, d - 1], ky_r.at[g, d - 1], at_y(my_y + d)
        )

    def unfold(slabs, rows):
        half = slabs.shape[2]
        return jnp.concatenate(
            [slabs[:, 0:rows].reshape(hd, half), slabs[:, rows : 2 * rows].reshape(hd, half)], axis=1
        )

    slice_rows = hd // nz

    def own_keys(g):
        each(1, nz, lambda d: first_back(g, d).wait_recv())
        at = slice(g * group_wide, (g + 1) * group_wide)
        before = unfold(gcar[g], slice_rows)
        gc[g] = before
        high, low = split(v_ref[...])
        carried_k = dot(high, before, NN) + dot(low, before, NN) + inner[:, at]
        for i in range(group_wide // hd):
            m = g * (group_wide // hd) + i
            kgl[g, :, i * hd : (i + 1) * hd] = (
                column(1, m) * carried_k[:, i * hd : (i + 1) * hd]
            ).astype(BF16)
        for d in range(1, ny):
            key_rows(g, d).start()

    own_keys(0)
    each(1, nh, lambda d: token_share(d).wait_recv())
    for d in range(1, ny):
        tkt[:, d * count : (d + 1) * count] = tk[d - 1].T

    def second_out(g, d):
        return scan_out(ksend.at[g], kin.at[g], ka_s.at[g], ka_r.at[g], d)

    def second_back(g, d):
        return scan_out(kmid_low.at[g], kcar.at[g], kb_s.at[g], kb_r.at[g], d)

    def second_middle(g, d):
        return scan_middle(kback.at[g], ktot.at[g], kt_s.at[g], kt_r.at[g], d)

    def row_pieces(d):
        y = lax.rem(my_y - d + ny, ny)
        at = pl.ds(y * nz, nz)
        return copy(wall.at[at], wall.at[at], wy_s.at[d - 1], wy_r.at[d - 1], at_y(my_y + d))

    for d in range(1, ny):
        row_pieces(d).wait_recv()
    val_t = split(v_ref[...].T)
    for g in range(groups):
        at = slice(g * group_wide, (g + 1) * group_wide)
        keys = dot(tok[...], wall[:, :, at].reshape(width, group_wide), NN)
        for i in range(group_wide // hd):
            m = g * (group_wide // hd) + i
            mk_h[:, m * hd : (m + 1) * hd], mk_l[:, m * hd : (m + 1) * hd] = split(
                column(1, m) * keys[:, i * hd : (i + 1) * hd]
            )
        local = dot3(val_t, (mk_h[:, at], mk_l[:, at]), NN)
        ksend[g] = jnp.concatenate(
            [
                local[:, 0 : group_wide // 2].reshape(nz, slice_rows, group_wide // 2),
                local[:, group_wide // 2 :].reshape(nz, slice_rows, group_wide // 2),
            ],
            axis=1,
        ).astype(BF16)
        each(1, nz, lambda d: second_out(g, d).start())
        kin[g, my_z] = ksend[g, my_z]

    own_keys(1)

    def flow(run, s, g):
        side, base, hops = reduce_runs[run]
        to = at_z(my_z + side * (1 if s < hops else base + 1))
        return copy(
            stage.at[run, s - 1, g], land.at[run, s - 1, g],
            rs_s.at[run, s - 1, g], rs_r.at[run, s - 1, g], to,
        )

    def target(run, s):
        side, base, hops = reduce_runs[run]
        return lax.rem(my_z + side * (base + hops - s + 1) + nz, nz)

    def enter(g):
        for d in range(1, ny):
            key_rows(g, d).wait_recv()
        product = dot(tkt[:, 0:count], kgl[g], NN)
        for d in range(1, ny):
            product = product + dot(tkt[:, d * count : (d + 1) * count], kgl_in[g, d - 1], NN)
        prod[g] = product.reshape(prod.shape[1:])
        for run in range(len(reduce_runs)):
            stage[run, 0, g] = prod[g, target(run, 1)]
            flow(run, 1, g).start()

    def reduce_step(g, s):
        for run in range(len(reduce_runs)):
            if s <= reduce_runs[run][2]:
                flow(run, s - 1, g).wait_recv()
                stage[run, s - 1, g] = land[run, s - 2, g] + prod[g, target(run, s)]
                flow(run, s, g).start()

    def reduce_end(g):
        done = prod[g, my_z]
        for run in range(len(reduce_runs)):
            hops = reduce_runs[run][2]
            flow(run, hops, g).wait_recv()
            done = done + land[run, hops - 1, g]
        for i in range(group_wide // hd):
            kg_out[:, g * (group_wide // hd) + i, :] = done[:, i * hd : (i + 1) * hd]

    def second_totals(g):
        each(1, nz, lambda d: second_out(g, d).wait_recv())
        kback[g] = sweep(kin.at[g], kmid.at[g], False)
        for d in range(1, ny):
            second_middle(g, d).start()

    def second_send_back(g):
        for d in range(1, ny):
            second_middle(g, d).wait_recv()
        extra = extra_of(ktot.at[g], False)
        for z in range(nz):
            kmid_low[g, z] = (kmid[g, z] + extra).astype(BF16)
        each(1, nz, lambda d: second_back(g, d).start())
        kcar[g, my_z] = kmid_low[g, my_z]

    def value_part():
        dout2 = split(do_ref[...])
        mk2 = (mk_h[...], mk_l[...])
        mixed = jnp.where(places_t >= places_s, dot3(mk2, (lift_h[...], lift_l[...]), NT), 0.0)
        total = dot3(split(mixed), dout2, NN)
        for g in range(groups):
            at = slice(g * group_wide, (g + 1) * group_wide)
            total = total + dot(mk2[0][:, at], gc[g], NT) + dot(mk2[1][:, at], gc[g], NT)
        vg_out[...] = total
        inner[...] = dot3((sc_h[...], sc_l[...]), mk2, NN)

    def gate_share(d):
        return copy(gate, gate_in.at[d - 1], gp_s.at[d - 1], gp_r.at[d - 1], at_head(head + d))

    def query_part():
        for g in range(groups):
            each(1, nz, lambda d: second_back(g, d).wait_recv())
        dout2 = split(do_ref[...])
        before = jnp.concatenate([unfold(kcar[g], slice_rows) for g in range(groups)], axis=1)
        state = dot(dout2[0], before, NN) + dot(dout2[1], before, NN) + inner[...]
        scaled_q = q_ref[...] * scale
        query = jnp.zeros((count, hd), F32)
        picks = [jnp.zeros((count, 1), F32), jnp.zeros((count, 1), F32)]
        for m in range(mem):
            here = state[:, m * hd : (m + 1) * hd]
            query = query + column(0, m) * here
            gradient = jnp.sum(scaled_q * here, axis=1, keepdims=True)
            for j in range(2):
                picks[j] = picks[j] + column(2 + j, m) * gradient
        qg_out[...] = scale * query
        lanes = lax.broadcasted_iota(jnp.int32, (count, hd), 1)
        spreaded = jnp.where(lanes == 0, picks[0], jnp.where(lanes == 1, picks[1], 0.0))
        gate[...] = spreaded.T[0:8, :]
        each(1, nh, lambda d: gate_share(d).start())

    def reduce_from(g, lower, upper):
        for s in range(lower, min(upper, reduce_longest) + 1):
            reduce_step(g, s)

    enter(0)
    second_totals(0)
    reduce_from(0, 2, 2)
    enter(1)
    second_totals(1)
    second_send_back(0)
    reduce_from(0, 3, 3)
    reduce_from(1, 2, 2)
    second_send_back(1)
    reduce_from(0, 4, reduce_longest)
    reduce_from(1, 3, reduce_longest)
    value_part()
    query_part()
    for g in range(groups):
        reduce_end(g)

    each(1, nh, lambda d: gate_share(d).wait_recv())
    total = gate[...]
    for d in range(1, nh):
        total = total + gate_in[d - 1]
    gg_out[...] = total[0:2, :]

    for run, (_, _, hops) in enumerate(spread_runs):
        for k in range(1, hops + 1):
            hop(run, k).wait_send()
    for run, (_, _, hops) in enumerate(reduce_runs):
        for s in range(1, hops + 1):
            for g in range(groups):
                flow(run, s, g).wait_send()
    for d in range(1, ny):
        row_pieces(d).wait_send()
        token_rows(d).wait_send()
        for g in range(groups):
            second_middle(g, d).wait_send()
            first_middle(g, d).wait_send()
            key_rows(g, d).wait_send()

    def sent(d):
        for g in range(groups):
            second_out(g, d).wait_send()
            second_back(g, d).wait_send()
            first_out(g, d).wait_send()
            first_back(g, d).wait_send()

    each(1, nz, sent)

    def shared(d):
        token_share(d).wait_send()
        gate_share(d).wait_send()

    each(1, nh, shared)


def on_device(rows, tokens, queries, values, dout, key_weight, routing, gates):
    count, width = tokens.shape
    depth, mem, hd = key_weight.shape
    contexts, nh = lax.axis_size("ctx"), lax.axis_size("head")
    ny, nz = rows, contexts // rows
    wide = mem * hd
    scale = 1.0 / math.sqrt(hd * count * contexts)
    half = nz // 2
    dma = pltpu.SemaphoreType.DMA
    rows_z = hd // nz
    slab = (2, nz, rows_z, wide // 2)
    low_slab = (2, nz, 2 * rows_z, wide // 4)
    first_scan = [
        pltpu.VMEM(slab, F32),
        pltpu.VMEM(slab, F32),
        pltpu.VMEM(slab, F32),
        pltpu.VMEM((2, ny - 1) + slab[2:], F32),
        pltpu.VMEM((2,) + slab[2:], F32),
        pltpu.VMEM(low_slab, BF16),
        pltpu.VMEM(low_slab, BF16),
    ]
    second_scan = [
        pltpu.VMEM(low_slab, BF16),
        pltpu.VMEM(low_slab, BF16),
        pltpu.VMEM(low_slab, F32),
        pltpu.VMEM((2, ny - 1) + low_slab[2:], F32),
        pltpu.VMEM((2,) + low_slab[2:], F32),
        pltpu.VMEM(low_slab, BF16),
        pltpu.VMEM(low_slab, BF16),
    ]
    first_sems = [dma((2, nz - 1))] * 2 + [dma((2, ny - 1))] * 2 + [dma((2, nz - 1))] * 2
    scratch = (
        [
            pltpu.VMEM((count, width), BF16),
            pltpu.VMEM((count, hd), F32),
            pltpu.VMEM((count, hd), F32),
            pltpu.VMEM((count, hd), F32),
            pltpu.VMEM((depth, mem, hd), BF16),
            pltpu.VMEM((depth, wide), BF16),
            pltpu.VMEM((2, count), jnp.int32),
            pltpu.VMEM((2, count), F32),
            dma((7,)),
            pltpu.VMEM((contexts, depth, wide), BF16),
            pltpu.VMEM((ny - 1, count, width // ny), BF16),
            pltpu.VMEM((width // ny, ny * count), BF16),
            pltpu.VMEM((2, count, wide // 2), BF16),
            pltpu.VMEM((2, ny - 1, count, wide // 2), BF16),
            pltpu.VMEM((count, wide), BF16),
            pltpu.VMEM((count, wide), BF16),
            pltpu.VMEM((count, wide), BF16),
            pltpu.VMEM((count, wide), BF16),
            pltpu.VMEM((count, 128), F32),
        ]
        + first_scan
        + second_scan
        + [
            pltpu.VMEM((2, nz, depth, wide // 2), F32),
            pltpu.VMEM((4, half, 2, depth, wide // 2), F32),
            pltpu.VMEM((4, half, 2, depth, wide // 2), F32),
            pltpu.VMEM((8, count), F32),
            pltpu.VMEM((nh - 1, 8, count), F32),
            pltpu.VMEM((count, count), BF16),
            pltpu.VMEM((count, count), BF16),
            pltpu.VMEM((count, wide), F32),
            pltpu.VMEM((2, hd, wide // 2), BF16),
        ]
        + [dma((4, half))] * 2
        + [dma((ny - 1,))] * 4
        + [dma((nh - 1,))] * 2
        + first_sems
        + first_sems
        + [dma((2, ny - 1))] * 2
        + [dma((4, half, 2))] * 2
        + [dma((nh - 1,))] * 2
    )
    vmem = pl.BlockSpec(memory_space=pltpu.VMEM)
    anywhere = pl.BlockSpec(memory_space=pl.ANY)
    key_grad, query_grad, value_grad, gate_grad = pl.pallas_call(
        functools.partial(kernel, (ny, nz, nh, mem, hd, scale)),
        out_shape=(
            jax.ShapeDtypeStruct((depth, mem, hd), F32),
            jax.ShapeDtypeStruct((count, hd), F32),
            jax.ShapeDtypeStruct((count, hd), F32),
            jax.ShapeDtypeStruct((2, count), F32),
        ),
        in_specs=[anywhere] * 7,
        out_specs=(vmem,) * 4,
        scratch_shapes=scratch,
        compiler_params=pltpu.CompilerParams(
            collective_id=0, has_side_effects=True, vmem_limit_bytes=56 * 1024 * 1024
        ),
    )(tokens, queries, values, dout, key_weight, routing.T, gates.T)
    return key_grad, query_grad, value_grad, gate_grad.T


def solution(mesh, rows=4):
    return jax.shard_map(
        functools.partial(on_device, rows),
        mesh=mesh,
        in_specs=(
            P("ctx", None),
            P("ctx", "head"),
            P("ctx", "head"),
            P("ctx", "head"),
            P("ctx", None, "head"),
            P("ctx", None),
            P("ctx", None),
        ),
        out_specs=(P("ctx", None, "head"), P("ctx", "head"), P("ctx", "head"), P("ctx", None)),
        check_vma=False,
    )
```
